256 devices in a mesh: grp: 8 (over y, core), sub: 32 (over x, z).
Axes of the slice: x: 4, y: 4, z: 8, core: 2. Of those that a mesh axis runs over, the one named last changes fastest.
Arguments:
- cluster_pos: float32 [3, 4096], P(None, 'sub'), may hold values from -3 to 3
- cluster_vel: float32 [3, 4096], P(None, 'sub'), may hold values from -15 to 15
- cluster_mass: float32 [4096], P('sub'), may hold values from 3 to 60
- galaxy_pos: float32 [3, 131072], P(None, ('grp', 'sub')), may hold values from -1 to 7
- galaxy_vel: float32 [3, 131072], P(None, ('grp', 'sub')), may hold values from -3 to 3
- galaxy_kind: int32 [131072], P(('grp', 'sub')), may hold values from 0 to 3
- species_mass: float32 [4], replicated, may hold values from 10 to 80
Outputs:
- cluster_pos_out: float32 [3, 4096], P(None, 'sub')
- cluster_vel_out: float32 [3, 4096], P(None, 'sub')
- galaxy_pos_out: float32 [3, 131072], P(None, ('grp', 'sub'))
- galaxy_vel_out: float32 [3, 131072], P(None, ('grp', 'sub'))
The draws below stay inside these ranges and needn't reach their ends.
All inputs are finite; a program needn't handle non-finite values.
Results may differ from the reference program's by a relative error of at most 0.0003.
Values sent between devices are 32-bit elements; how exact they have to be, the bound alone decides.
A program may use at most 64 MiB of HBM per device.

```python
import math
import jax
import jax.numpy as jnp
import numpy as np
from jax import lax

G_DEV = 512
SUBSTEPS = 8
KINDS = 4
NC = 4096
NG = 131072


def place_ends(values, own_key, low, high):
    shape = values.shape
    spot = [jax.random.randint(jax.random.fold_in(own_key, axis), (), 0, shape[axis]) for axis in range(len(shape))]
    values = values.at[tuple(spot)].set(low)
    longest = shape.index(max(shape))
    spot[longest] = (spot[longest] + 1) % shape[longest]
    return values.at[tuple(spot)].set(high)


def level_of(key, extent, cuts, least, top_value):
    factor_of = 1.0
    for dim, parts in cuts:
        draws = jax.random.uniform(jax.random.fold_in(jax.random.fold_in(key, 6), dim), (parts,), jnp.float32, least / len(cuts), top_value / len(cuts))
        factor_of = factor_of * jnp.repeat(jnp.exp(draws), extent[dim] // parts).reshape((-1,) + (1,) * (len(extent) - 1 - dim))
    return factor_of


def rank_table(number_of, lean):
    loads = [(1 << 20) // math.isqrt(rank ** lean) + 1 for rank in range(1, number_of + 1)]
    spread = 1 + sum(loads) // (1 << 30)
    return np.cumsum(np.array([max(1, weight // spread) for weight in loads]))


def ranked(stream_key, extent, count, lean):
    listing = rank_table(count, lean)
    ticket = jax.random.randint(jax.random.fold_in(stream_key, 1), extent, 0, int(listing[count - 1]))
    grade = jnp.searchsorted(jnp.asarray(listing, jnp.int32), ticket, side="right")
    return jax.random.permutation(jax.random.fold_in(stream_key, 2), count)[grade].astype(jnp.int32)


def normal_values(key, extent, width, limit, split=(), held_as=jnp.bfloat16):
    drawn = jax.random.normal(key, extent, jnp.float32) * width
    if len(split) > 0:
        drawn = level_of(key, extent, split, -0.22, 0.18) * drawn
    return jnp.clip(drawn, min=-limit, max=limit).astype(held_as)


def setup_inputs(seed: int = 0) -> dict:
    key_of = jax.random.split(jax.random.key(seed), 8)
    return {
        "cluster_pos": normal_values(key_of[0], (3, NC), 0.5, 3.0, ((1, 32),), jnp.float32),
        "cluster_vel": normal_values(key_of[1], (3, NC), 2.5, 15.0, ((1, 32),), jnp.float32),
        "cluster_mass": jnp.clip(jnp.exp(math.log(60.0) - 2.9957323 * jax.random.uniform(key_of[2], (NC,), jnp.float32) ** level_of(key_of[2], (NC,), ((0, 32),), -0.2, 0.2)), 3.0, 60.0),
        "galaxy_pos": jnp.clip(-1.0 + 8.0 * jax.random.uniform(key_of[3], (3, NG), jnp.float32) ** level_of(key_of[3], (3, NG), ((1, 256),), -0.2, 0.2), -1.0, 7.0),
        "galaxy_vel": normal_values(key_of[4], (3, NG), 0.5, 3.0, ((1, 256),), jnp.float32),
        "galaxy_kind": place_ends(ranked(key_of[5], (NG,), KINDS, 2), jax.random.fold_in(key_of[5], 3), 0, KINDS - 1).astype(jnp.int32),
        "species_mass": jnp.clip(jnp.exp(jax.random.uniform(key_of[6], (KINDS,), jnp.float32, math.log(10.0), math.log(80.0))), 10.0, 80.0),
    }


step_time = 0.5
bridge_soft = 0.01
cluster_soft = 0.0025
tile_limit = 524288

def pick_block(target_count, source_count):
    tile_size = target_count
    while tile_size > 1 and (tile_size * source_count > tile_limit or target_count % tile_size != 0):
        tile_size = tile_size // 2
    return tile_size

def field(targets, sources, masses, soften):
    target_count = targets.shape[1]
    tile_size = pick_block(target_count, sources.shape[1])

    def one_tile(target_tile):
        separation = sources[:, None, :] - target_tile[:, :, None]
        distance = lax.optimization_barrier(jnp.sum(separation * separation, axis=0)) + soften
        inverse = lax.rsqrt(distance)
        weight = masses[None, :] * inverse * inverse * inverse
        return lax.optimization_barrier(jnp.sum(separation * weight[None], axis=2))
    stacked = targets.reshape(3, target_count // tile_size, tile_size).transpose(1, 0, 2)
    result = lax.map(one_tile, stacked)
    return result.transpose(1, 0, 2).reshape(3, target_count)

def rates(target_pos, target_vel, source_pos, source_vel, masses, soften):
    target_count = target_pos.shape[1]
    tile_size = pick_block(target_count, source_pos.shape[1])

    def one_tile(target_tile):
        separation = source_pos[:, None, :] - target_tile[:3, :, None]
        closing = source_vel[:, None, :] - target_tile[3:, :, None]
        distance = lax.optimization_barrier(jnp.sum(separation * separation, axis=0)) + soften
        inverse = lax.rsqrt(distance)
        weight = masses[None, :] * inverse * inverse * inverse
        radial = 3.0 * lax.optimization_barrier(jnp.sum(separation * closing, axis=0)) / distance
        acceleration = lax.optimization_barrier(jnp.sum(separation * weight[None], axis=2))
        jerk_rate = lax.optimization_barrier(jnp.sum((closing - radial[None] * separation) * weight[None], axis=2))
        return jnp.concatenate([acceleration, jerk_rate], axis=0)
    stacked = jnp.concatenate([target_pos, target_vel], axis=0)
    stacked = stacked.reshape(6, target_count // tile_size, tile_size).transpose(1, 0, 2)
    result = lax.map(one_tile, stacked)
    return result.transpose(1, 0, 2).reshape(6, target_count)

def galaxy_pull(targets, galaxy_positions, body_mass):
    blocks = NG // G_DEV
    block_pos = galaxy_positions.reshape(3, blocks, G_DEV).transpose(1, 0, 2)
    block_mass = body_mass.reshape(blocks, G_DEV)

    def add_block(running, item):
        return (running + field(targets, item[0], item[1], bridge_soft), None)
    running, unused = lax.scan(add_block, jnp.zeros((3, targets.shape[1]), jnp.float32), (block_pos, block_mass))
    return running

def reference(cluster_pos, cluster_vel, cluster_mass, galaxy_pos, galaxy_vel, galaxy_kind, species_mass):
    star_mass = cluster_mass / NC
    species = jnp.arange(KINDS, dtype=jnp.int32)
    body_mass = lax.optimization_barrier(jnp.sum(jnp.where(galaxy_kind[None, :] == species[:, None], species_mass[:, None], 0.0), axis=0)) / NG
    half_step = step_time / 2.0
    star_vel = cluster_vel + half_step * galaxy_pull(cluster_pos, galaxy_pos, body_mass)
    body_vel = galaxy_vel + half_step * field(galaxy_pos, cluster_pos, star_mass, bridge_soft)
    body_pos = galaxy_pos + step_time * body_vel
    substep_time = step_time / SUBSTEPS
    positions, velocity = (cluster_pos, star_vel)
    both = rates(positions, velocity, positions, velocity, star_mass, cluster_soft)
    acceleration, jerk_rate = (both[:3], both[3:])
    for substep in range(SUBSTEPS):
        guess_pos = positions + substep_time * (velocity + substep_time * (acceleration / 2.0 + substep_time * jerk_rate / 6.0))
        guess_vel = velocity + substep_time * (acceleration + substep_time * jerk_rate / 2.0)
        fresh = rates(guess_pos, guess_vel, guess_pos, guess_vel, star_mass, cluster_soft)
        new_acc, new_jerk = (fresh[:3], fresh[3:])
        new_vel = velocity + substep_time / 2.0 * (acceleration + new_acc) + substep_time * substep_time / 12.0 * (jerk_rate - new_jerk)
        new_pos = positions + substep_time / 2.0 * (velocity + new_vel) + substep_time * substep_time / 12.0 * (acceleration - new_acc)
        positions, velocity, acceleration, jerk_rate = (new_pos, new_vel, new_acc, new_jerk)
    final_vel = velocity + half_step * galaxy_pull(positions, body_pos, body_mass)
    final_body_vel = body_vel + half_step * field(body_pos, positions, star_mass, bridge_soft)
    return (positions, final_vel, body_pos, final_body_vel)
```

```python
import functools

import jax
import jax.numpy as jnp
from jax import lax
from jax.experimental import pallas as pl
from jax.experimental.pallas import tpu as pltpu
from jax.sharding import PartitionSpec as P

SUBSTEPS = 8
STEP_TIME = 0.5
HALF = STEP_TIME / 2.0
BRIDGE_SOFT = 0.01
CLUSTER_SOFT = 0.0025
F32 = jnp.float32
MESH = pl.DeviceIdType.MESH
LANES = 128


def columns(tile):
    pad = jnp.zeros((LANES - tile.shape[0], LANES), F32)
    return jnp.concatenate([tile, pad], axis=0).T


def kernel(
    sizes,
    cpos, cvel, cmass, gpos, gvel, gkind, species,
    opos, ovel, ogpos, ogvel,
    stars, wide, parts, landed, ring, ring_out, swap, landed2, ring2, ring2_out,
    target, acc6, accp, body, bvel, state,
    sa, ra, sr, rr, sz, rz, se, re, sr2, rr2, sg, rg,
):
    G, X, Z, NB, GB = sizes
    total_bodies = GB * LANES * G * NB
    total_stars = NB * LANES
    g, s = lax.axis_index("grp"), lax.axis_index("sub")
    x, z = s // Z, s % Z
    q = x * G + g
    team = lambda p: {"grp": p % G, "sub": (p // G) * Z + z}

    def copy(src, dst, send, recv, dev):
        return pltpu.make_async_remote_copy(
            src_ref=src, dst_ref=dst, send_sem=send, recv_sem=recv,
            device_id=dev, device_id_type=MESH,
        )

    def wait_blocks(buf, n, sem):
        part = buf.at[pl.ds(0, n)]
        pltpu.make_async_copy(part, part, sem).wait()

    barrier = pltpu.get_barrier_semaphore()

    def greet_sub(d, _):
        pl.semaphore_signal(
            barrier, inc=1, device_id={"grp": g, "sub": (s + d) % NB}, device_id_type=MESH
        )
        return 0

    def greet_team(d, _):
        gd = (g + 1 + d // X) % G
        xd = d % X
        pl.semaphore_signal(
            barrier, inc=1, device_id={"grp": gd, "sub": xd * Z + z}, device_id_type=MESH
        )
        return 0

    lax.fori_loop(1, NB, greet_sub, 0)
    lax.fori_loop(0, (G - 1) * X, greet_team, 0)

    stars[s] = jnp.concatenate(
        [cpos[...], cvel[...], cmass[...] / total_stars, jnp.zeros((1, LANES), F32)], axis=0
    )
    kinds = gkind[...]
    mass = jnp.zeros(kinds.shape, F32)
    for kind in range(species.shape[0]):
        mass = mass + jnp.where(kinds == kind, species[kind], 0.0)
    body[...] = mass / total_bodies

    def widen(positions):
        for b in range(GB):
            at = slice(b * LANES, (b + 1) * LANES)
            tile = jnp.concatenate(
                [positions[:, at], body[:, at], jnp.zeros((4, LANES), F32)], axis=0
            )
            cols = columns(tile)
            for i in range(4):
                wide[i, at, :] = jnp.broadcast_to(cols[:, i : i + 1], (LANES, LANES))

    widen(gpos[...])
    pl.semaphore_wait(barrier, (NB - 1) + (G - 1) * X)

    def send_stars(d, _):
        copy(stars.at[s], stars.at[s], sa, ra, {"grp": g, "sub": (s + d) % NB}).start()
        return 0

    lax.fori_loop(1, NB, send_stars, 0)
    wait_blocks(stars, NB - 1, ra)

    def pull(rows):
        at = [jnp.broadcast_to(r, (8, LANES)) for r in rows]

        def step(i, acc):
            here = pl.ds(pl.multiple_of(i * 8, 8), 8)
            d = [wide[c, here, :] - at[c] for c in range(3)]
            r2 = d[0] * d[0] + d[1] * d[1] + d[2] * d[2] + BRIDGE_SOFT
            inv = lax.rsqrt(r2)
            w = wide[3, here, :] * (inv * inv * inv)
            return tuple(acc[c] + w * d[c] for c in range(3))

        zero = jnp.zeros((8, LANES), F32)
        acc = lax.fori_loop(0, GB * LANES // 8, step, (zero, zero, zero), unroll=8)
        return jnp.concatenate(
            [jnp.sum(a, axis=0, keepdims=True) for a in acc] + [jnp.zeros((1, LANES), F32)], axis=0
        )

    def push(first, position_row):
        here = pl.ds(pl.multiple_of(first, 16), 16)
        at = [wide[c, here, :] for c in range(3)]

        def step(b, acc):
            d = [position_row(b, c) - at[c] for c in range(3)]
            r2 = d[0] * d[0] + d[1] * d[1] + d[2] * d[2] + BRIDGE_SOFT
            inv = lax.rsqrt(r2)
            w = stars[b, 6:7, :] * (inv * inv * inv)
            return tuple(acc[c] + w * d[c] for c in range(3))

        zero = jnp.zeros((16, LANES), F32)
        acc = lax.fori_loop(0, NB, step, (zero, zero, zero), unroll=4)
        for c in range(3):
            accp[c, here, :] = acc[c]

    def pushed():
        rows = []
        for c in range(3):
            rows.append(
                jnp.concatenate(
                    [
                        jnp.sum(accp[c, b * LANES : (b + 1) * LANES, :].T, axis=0, keepdims=True)
                        for b in range(GB)
                    ],
                    axis=1,
                )
            )
        return jnp.concatenate(rows, axis=0)

    def first_pull(b, _):
        p = (q + 1 + b) % NB
        parts[p] = pull([stars[p, c : c + 1, :] for c in range(3)])

        @pl.when(b < NB - 1)
        def _():
            copy(parts.at[p], landed.at[q], sr, rr, team(p)).start()

        return 0

    lax.fori_loop(0, NB, first_pull, 0)
    landed[q] = parts[q]
    wait_blocks(landed, NB - 1, rr)
    ring_out[...] = jnp.sum(landed[...], axis=0)

    def send_ring(d, _):
        copy(ring_out, ring.at[z], sz, rz, {"grp": g, "sub": x * Z + (z + d) % Z}).start()
        return 0

    lax.fori_loop(1, Z, send_ring, 0)
    ring[z] = ring_out[...]
    wait_blocks(ring, Z - 1, rz)
    mine = stars[q]
    state[0:3, :] = mine[0:3]
    state[3:6, :] = mine[3:6] + HALF * jnp.sum(ring[...], axis=0)[0:3]
    state[6:12, :] = jnp.zeros((6, LANES), F32)

    two = jnp.zeros((2, LANES), F32)

    def send_swap(par, rows):
        swap[par, q] = jnp.concatenate([rows, two], axis=0)

        def one(d, _):
            p = (q + d) % NB
            copy(swap.at[par, q], swap.at[par, q], se.at[par], re.at[par], team(p)).start()
            return 0

        lax.fori_loop(1, NB, one, 0)

    def wait_swap(par, sem):
        part = swap.at[par, pl.ds(0, NB - 1)]
        pltpu.make_async_copy(part, part, sem.at[par]).wait()

    def rates(par):
        def rows16(i, _):
            here = pl.ds(pl.multiple_of(i * 16, 16), 16)
            at = [target[c, here, :] for c in range(6)]

            def step(b, acc):
                d = [swap[par, b, c : c + 1, :] - at[c] for c in range(3)]
                v = [swap[par, b, c + 3 : c + 4, :] - at[c + 3] for c in range(3)]
                r2 = d[0] * d[0] + d[1] * d[1] + d[2] * d[2] + CLUSTER_SOFT
                rv = d[0] * v[0] + d[1] * v[1] + d[2] * v[2]
                inv = lax.rsqrt(r2)
                i2 = inv * inv
                w = stars[b, 6:7, :] * (inv * i2)
                u = w * (3.0 * i2 * rv)
                return tuple(acc[c] + w * d[c] for c in range(3)) + tuple(
                    acc[3 + c] + (w * v[c] - u * d[c]) for c in range(3)
                )

            zero = jnp.zeros((16, LANES), F32)
            acc = lax.fori_loop(0, NB, step, (zero,) * 6, unroll=4)
            for c in range(6):
                acc6[c, here, :] = acc[c]
            return 0

        lax.fori_loop(0, LANES // 16, rows16, 0)
        return jnp.concatenate(
            [jnp.sum(acc6[c].T, axis=0, keepdims=True) for c in range(6)], axis=0
        )

    h = STEP_TIME / SUBSTEPS

    def substep(k, _):
        par = k % 2
        first = k == 0
        xs, v, a, j = state[0:3, :], state[3:6, :], state[6:9, :], state[9:12, :]
        guess = jnp.concatenate(
            [
                xs + h * (v + h * (a / 2.0 + h * j / 6.0)),
                v + h * (a + h * j / 2.0),
            ],
            axis=0,
        )
        rows = jnp.where(first, state[0:6, :], guess)

        @pl.when(k >= 2)
        def _():
            wait_swap(par, se)

        send_swap(par, rows)
        cols = columns(jnp.concatenate([rows, two], axis=0))
        for c in range(6):
            target[c] = jnp.broadcast_to(cols[:, c : c + 1], (LANES, LANES))

        @pl.when(k < SUBSTEPS)
        def _():
            count = GB * LANES // SUBSTEPS

            def some(i, _):
                push(k * count + i * 16, lambda b, c: stars[b, c : c + 1, :])
                return 0

            lax.fori_loop(0, count // 16, some, 0)

        wait_swap(par, re)
        fresh = rates(par)
        a1, j1 = fresh[0:3], fresh[3:6]
        v1 = v + h / 2.0 * (a + a1) + h * h / 12.0 * (j - j1)
        x1 = xs + h / 2.0 * (v + v1) + h * h / 12.0 * (a - a1)
        state[0:3, :] = jnp.where(first, xs, x1)
        state[3:6, :] = jnp.where(first, v, v1)
        state[6:9, :] = a1
        state[9:12, :] = j1
        return 0

    lax.fori_loop(0, SUBSTEPS + 1, substep, 0)

    last = (SUBSTEPS + 1) % 2
    wait_swap(last, se)
    send_swap(last, state[0:6, :])

    velocity = gvel[...] + HALF * pushed()
    bvel[...] = velocity
    moved = gpos[...] + STEP_TIME * velocity
    ogpos[...] = moved
    widen(moved)
    wait_blocks(parts, NB - 1, sr)
    wait_swap(last, re)
    opos[...] = swap[last, s, 0:3, :]

    def second_pull(b, _):
        p = (s + 1 + b) % NB
        parts[p] = pull([swap[last, p, c : c + 1, :] for c in range(3)])

        @pl.when(b < NB - 1)
        def _():
            copy(parts.at[p], landed2.at[s], sr2, rr2, {"grp": g, "sub": p}).start()

        return 0

    lax.fori_loop(0, NB, second_pull, 0)
    landed2[s] = parts[s]

    def some_push(i, _):
        push(i * 16, lambda b, c: swap[last, b, c : c + 1, :])
        return 0

    count = GB * LANES // 16
    lax.fori_loop(0, count // 2, some_push, 0)
    wait_blocks(landed2, NB - 1, rr2)
    ring2_out[...] = jnp.sum(landed2[...], axis=0)

    def send_ring2(d, _):
        copy(ring2_out, ring2.at[g], sg, rg, {"grp": (g + d) % G, "sub": s}).start()
        return 0

    lax.fori_loop(1, G, send_ring2, 0)
    ring2[g] = ring2_out[...]
    lax.fori_loop(count // 2, count, some_push, 0)
    ogvel[...] = bvel[...] + HALF * pushed()
    wait_blocks(ring2, G - 1, rg)
    ovel[...] = swap[last, s, 3:6, :] + HALF * jnp.sum(ring2[...], axis=0)[0:3]

    wait_blocks(stars, NB - 1, sa)
    wait_blocks(ring, Z - 1, sz)
    wait_swap(1 - last, se)
    wait_swap(last, se)
    wait_blocks(landed2, NB - 1, sr2)
    wait_blocks(ring2, G - 1, sg)


def solution(mesh):
    G = mesh.shape["grp"]
    NB = mesh.shape["sub"]
    Z = G
    X = NB // Z

    def local(cpos, cvel, cmass, gpos, gvel, gkind, species):
        bodies = gpos.shape[1]
        GB = bodies // LANES
        vmem = pl.BlockSpec(memory_space=pltpu.VMEM)
        smem = pl.BlockSpec(memory_space=pltpu.SMEM)
        dma = pltpu.SemaphoreType.DMA
        return pl.pallas_call(
            functools.partial(kernel, (G, X, Z, NB, GB)),
            out_shape=(
                jax.ShapeDtypeStruct(cpos.shape, F32),
                jax.ShapeDtypeStruct(cpos.shape, F32),
                jax.ShapeDtypeStruct(gpos.shape, F32),
                jax.ShapeDtypeStruct(gpos.shape, F32),
            ),
            in_specs=[vmem] * 6 + [smem],
            out_specs=(vmem,) * 4,
            scratch_shapes=[
                pltpu.VMEM((NB, 8, LANES), F32),
                pltpu.VMEM((4, bodies, LANES), F32),
                pltpu.VMEM((NB, 4, LANES), F32),
                pltpu.VMEM((NB, 4, LANES), F32),
                pltpu.VMEM((Z, 4, LANES), F32),
                pltpu.VMEM((4, LANES), F32),
                pltpu.VMEM((2, NB, 8, LANES), F32),
                pltpu.VMEM((NB, 4, LANES), F32),
                pltpu.VMEM((G, 4, LANES), F32),
                pltpu.VMEM((4, LANES), F32),
                pltpu.VMEM((6, LANES, LANES), F32),
                pltpu.VMEM((6, LANES, LANES), F32),
                pltpu.VMEM((3, bodies, LANES), F32),
                pltpu.VMEM((1, bodies), F32),
                pltpu.VMEM((3, bodies), F32),
                pltpu.VMEM((16, LANES), F32),
                dma, dma, dma, dma, dma, dma,
                dma((2,)), dma((2,)),
                dma, dma, dma, dma,
            ],
            compiler_params=pltpu.CompilerParams(collective_id=0, has_side_effects=True),
        )(cpos, cvel, cmass.reshape(1, LANES), gpos, gvel, gkind.reshape(1, bodies), species)

    return jax.shard_map(
        local,
        mesh=mesh,
        in_specs=(
            P(None, "sub"),
            P(None, "sub"),
            P("sub"),
            P(None, ("grp", "sub")),
            P(None, ("grp", "sub")),
            P(("grp", "sub")),
            P(),
        ),
        out_specs=(
            P(None, "sub"),
            P(None, "sub"),
            P(None, ("grp", "sub")),
            P(None, ("grp", "sub")),
        ),
        check_vma=False,
    )
```

```python
import functools

import jax
import jax.numpy as jnp
from jax import lax
from jax.experimental import pallas as pl
from jax.experimental.pallas import tpu as pltpu
from jax.sharding import PartitionSpec as P

SUBSTEPS = 8
STEP_TIME = 0.5
HALF = STEP_TIME / 2.0
BRIDGE_SOFT = 0.01
CLUSTER_SOFT = 0.0025
F32 = jnp.float32
MESH = pl.DeviceIdType.MESH
LANES = 128


def ring_distance(d, n):
    return min(d % n, (-d) % n)


def chip_stages(X, Y):
    stages = [[] for _ in range(X // 2 + Y // 2 + 1)]
    for dx in range(X):
        for dy in range(Y):
            stages[ring_distance(dx, X) + ring_distance(dy, Y)].append((dx, dy))
    return stages


def columns(tile):
    pad = jnp.zeros((LANES - tile.shape[0], LANES), F32)
    return jnp.concatenate([tile, pad], axis=0).T


def kernel(
    sizes,
    cpos, cvel, cmass, gpos, gvel, gkind, species,
    opos, ovel, ogpos, ogvel,
    stars, wide, parts, landed, ring, ring_out, swap, landed2, ring2, ring2_out,
    target, acc6, accp, body, bvel, state,
    sa, ra, sr, rr, sz, rz, se, re, sr2, rr2, sg, rg,
):
    G, X, Z, NB, GB = sizes
    total_bodies = GB * LANES * G * NB
    total_stars = NB * LANES
    g, s = lax.axis_index("grp"), lax.axis_index("sub")
    x, z = s // Z, s % Z
    q = x * G + g
    team = lambda p: {"grp": p % G, "sub": (p // G) * Z + z}
    Y, y, core = G // 2, g // 2, g % 2
    stages = chip_stages(X, Y)
    chip_at = lambda dx, dy: ((x + dx) % X) * G + ((y + dy) % Y) * 2

    def copy(src, dst, send, recv, dev):
        return pltpu.make_async_remote_copy(
            src_ref=src, dst_ref=dst, send_sem=send, recv_sem=recv,
            device_id=dev, device_id_type=MESH,
        )

    def wait_blocks(buf, n, sem):
        part = buf.at[pl.ds(0, n)]
        pltpu.make_async_copy(part, part, sem).wait()

    barrier = pltpu.get_barrier_semaphore()

    def greet_sub(d, _):
        pl.semaphore_signal(
            barrier, inc=1, device_id={"grp": g, "sub": (s + d) % NB}, device_id_type=MESH
        )
        return 0

    def greet_team(d, _):
        gd = (g + 1 + d // X) % G
        xd = d % X
        pl.semaphore_signal(
            barrier, inc=1, device_id={"grp": gd, "sub": xd * Z + z}, device_id_type=MESH
        )
        return 0

    lax.fori_loop(1, NB, greet_sub, 0)
    lax.fori_loop(0, (G - 1) * X, greet_team, 0)

    stars[s] = jnp.concatenate(
        [cpos[...], cvel[...], cmass[...] / total_stars, jnp.zeros((1, LANES), F32)], axis=0
    )
    kinds = gkind[...]
    mass = jnp.zeros(kinds.shape, F32)
    for kind in range(species.shape[0]):
        mass = mass + jnp.where(kinds == kind, species[kind], 0.0)
    body[...] = mass / total_bodies

    def widen(positions):
        for b in range(GB):
            at = slice(b * LANES, (b + 1) * LANES)
            tile = jnp.concatenate(
                [positions[:, at], body[:, at], jnp.zeros((4, LANES), F32)], axis=0
            )
            cols = columns(tile)
            for i in range(4):
                wide[i, at, :] = jnp.broadcast_to(cols[:, i : i + 1], (LANES, LANES))

    widen(gpos[...])
    pl.semaphore_wait(barrier, (NB - 1) + (G - 1) * X)

    sub_stages = [
        [[(dx, dz) for dx in range(X)] for dz in sorted({st, (-st) % Z})] for st in range(Z // 2 + 1)
    ]
    sub_at = lambda dx, dz: ((x + dx) % X) * Z + (z + dz) % Z

    for st in reversed(range(len(sub_stages))):
        for group in sub_stages[st]:
            for dx, dz in group:
                if (dx, dz) != (0, 0):
                    copy(
                        stars.at[s], stars.at[s], sa, ra.at[st],
                        {"grp": g, "sub": sub_at(dx, dz)},
                    ).start()

    def pull(blocks):
        n = len(blocks)
        at = [[jnp.broadcast_to(r, (8, LANES)) for r in rows] for rows in blocks]

        def step(i, acc):
            here = pl.ds(pl.multiple_of(i * 8, 8), 8)
            body_at = [wide[c, here, :] for c in range(4)]
            out = []
            for k in range(n):
                d = [body_at[c] - at[k][c] for c in range(3)]
                r2 = d[0] * d[0] + d[1] * d[1] + d[2] * d[2] + BRIDGE_SOFT
                inv = lax.rsqrt(r2)
                w = body_at[3] * (inv * inv * inv)
                out.append(tuple(acc[k][c] + w * d[c] for c in range(3)))
            return tuple(out)

        zero = jnp.zeros((8, LANES), F32)
        acc = lax.fori_loop(0, GB * LANES // 8, step, ((zero,) * 3,) * n, unroll=8 // n)
        return [
            jnp.concatenate(
                [jnp.sum(a, axis=0, keepdims=True) for a in one]
                + [jnp.zeros((1, LANES), F32)],
                axis=0,
            )
            for one in acc
        ]

    def push(first, position_row):
        here = pl.ds(pl.multiple_of(first, 16), 16)
        at = [wide[c, here, :] for c in range(3)]

        def step(b, acc):
            d = [position_row(b, c) - at[c] for c in range(3)]
            r2 = d[0] * d[0] + d[1] * d[1] + d[2] * d[2] + BRIDGE_SOFT
            inv = lax.rsqrt(r2)
            w = stars[b, 6:7, :] * (inv * inv * inv)
            return tuple(acc[c] + w * d[c] for c in range(3))

        zero = jnp.zeros((16, LANES), F32)
        acc = lax.fori_loop(0, NB, step, (zero, zero, zero), unroll=4)
        for c in range(3):
            accp[c, here, :] = acc[c]

    def pushed():
        rows = []
        for c in range(3):
            rows.append(
                jnp.concatenate(
                    [
                        jnp.sum(accp[c, b * LANES : (b + 1) * LANES, :].T, axis=0, keepdims=True)
                        for b in range(GB)
                    ],
                    axis=1,
                )
            )
        return jnp.concatenate(rows, axis=0)

    for st, groups in enumerate(sub_stages):
        count = sum(len(group) for group in groups) - (1 if st == 0 else 0)
        wait_blocks(stars, count, ra.at[st])
        for group in groups:
            at = [sub_at(dx, dz) for dx, dz in group]
            done = pull([[stars[p, c : c + 1, :] for c in range(3)] for p in at])
            for p, value in zip(at, done):
                parts[p] = value

                @pl.when(p != q)
                def _():
                    copy(parts.at[p], landed.at[q], sr, rr, team(p)).start()

    landed[q] = parts[q]
    wait_blocks(landed, NB - 1, rr)
    ring_out[...] = jnp.sum(landed[...], axis=0)

    def send_ring(d, _):
        copy(ring_out, ring.at[z], sz, rz, {"grp": g, "sub": x * Z + (z + d) % Z}).start()
        return 0

    lax.fori_loop(1, Z, send_ring, 0)
    ring[z] = ring_out[...]
    wait_blocks(ring, Z - 1, rz)
    mine = stars[q]
    state[0:3, :] = mine[0:3]
    state[3:6, :] = mine[3:6] + HALF * jnp.sum(ring[...], axis=0)[0:3]
    state[6:12, :] = jnp.zeros((6, LANES), F32)

    two = jnp.zeros((2, LANES), F32)

    def send_swap(par, rows):
        swap[par, q] = jnp.concatenate([rows, two], axis=0)
        for st in reversed(range(len(stages))):
            for dx, dy in stages[st]:
                for dc in range(2):
                    if (dx, dy, dc) != (0, 0, 0):
                        p = chip_at(dx, dy) + (core + dc) % 2
                        copy(
                            swap.at[par, q], swap.at[par, q], se.at[par], re.at[par, st], team(p)
                        ).start()

    def wait_swap(par, sem, count):
        part = swap.at[par, pl.ds(0, count)]
        pltpu.make_async_copy(part, part, sem).wait()

    def wait_sent(par):
        wait_swap(par, se.at[par], NB - 1)

    def wait_stage(par, st):
        wait_swap(par, re.at[par, st], 2 * len(stages[st]) - (1 if st == 0 else 0))

    def rates_stage(par, st):
        blocks = [chip_at(dx, dy) + c for dx, dy in stages[st] for c in range(2)]

        def rows16(i, _):
            here = pl.ds(pl.multiple_of(i * 16, 16), 16)
            at = [target[c, here, :] for c in range(6)]
            if st == 0:
                acc = [jnp.zeros((16, LANES), F32)] * 6
            else:
                acc = [acc6[c, here, :] for c in range(6)]
            for b in blocks:
                d = [swap[par, b, c : c + 1, :] - at[c] for c in range(3)]
                v = [swap[par, b, c + 3 : c + 4, :] - at[c + 3] for c in range(3)]
                r2 = d[0] * d[0] + d[1] * d[1] + d[2] * d[2] + CLUSTER_SOFT
                rv = d[0] * v[0] + d[1] * v[1] + d[2] * v[2]
                inv = lax.rsqrt(r2)
                i2 = inv * inv
                w = stars[b, 6:7, :] * (inv * i2)
                u = w * (3.0 * i2 * rv)
                acc = [acc[c] + w * d[c] for c in range(3)] + [
                    acc[3 + c] + (w * v[c] - u * d[c]) for c in range(3)
                ]
            for c in range(6):
                acc6[c, here, :] = acc[c]
            return 0

        lax.fori_loop(0, LANES // 16, rows16, 0)

    def rates(par):
        for st in range(len(stages)):
            wait_stage(par, st)
            rates_stage(par, st)
        return jnp.concatenate(
            [jnp.sum(acc6[c].T, axis=0, keepdims=True) for c in range(6)], axis=0
        )

    h = STEP_TIME / SUBSTEPS

    def substep(k, _):
        par = k % 2
        first = k == 0
        xs, v, a, j = state[0:3, :], state[3:6, :], state[6:9, :], state[9:12, :]
        guess = jnp.concatenate(
            [
                xs + h * (v + h * (a / 2.0 + h * j / 6.0)),
                v + h * (a + h * j / 2.0),
            ],
            axis=0,
        )
        rows = jnp.where(first, state[0:6, :], guess)

        @pl.when(k >= 2)
        def _():
            wait_sent(par)

        send_swap(par, rows)
        cols = columns(jnp.concatenate([rows, two], axis=0))
        for c in range(6):
            target[c] = jnp.broadcast_to(cols[:, c : c + 1], (LANES, LANES))

        @pl.when(k < SUBSTEPS)
        def _():
            count = GB * LANES // SUBSTEPS

            def some(i, _):
                push(k * count + i * 16, lambda b, c: stars[b, c : c + 1, :])
                return 0

            lax.fori_loop(0, count // 16, some, 0)

        fresh = rates(par)
        a1, j1 = fresh[0:3], fresh[3:6]
        v1 = v + h / 2.0 * (a + a1) + h * h / 12.0 * (j - j1)
        x1 = xs + h / 2.0 * (v + v1) + h * h / 12.0 * (a - a1)
        state[0:3, :] = jnp.where(first, xs, x1)
        state[3:6, :] = jnp.where(first, v, v1)
        state[6:9, :] = a1
        state[9:12, :] = j1
        return 0

    lax.fori_loop(0, SUBSTEPS + 1, substep, 0)

    last = (SUBSTEPS + 1) % 2
    wait_sent(last)
    send_swap(last, state[0:6, :])

    velocity = gvel[...] + HALF * pushed()
    bvel[...] = velocity
    moved = gpos[...] + STEP_TIME * velocity
    ogpos[...] = moved
    widen(moved)
    wait_blocks(parts, NB - 1, sr)

    for st, chips in enumerate(stages):
        wait_stage(last, st)
        for at in range(0, len(chips), 2):
            some = [chip_at(dx, dy) + c for dx, dy in chips[at : at + 2] for c in range(2)]
            done = pull([[swap[last, p, c : c + 1, :] for c in range(3)] for p in some])
            for p, value in zip(some, done):
                parts[p] = value

                @pl.when(p != s)
                def _():
                    copy(parts.at[p], landed2.at[s], sr2, rr2, {"grp": g, "sub": p}).start()

    opos[...] = swap[last, s, 0:3, :]
    landed2[s] = parts[s]

    def some_push(i, _):
        push(i * 16, lambda b, c: swap[last, b, c : c + 1, :])
        return 0

    count = GB * LANES // 16
    lax.fori_loop(0, count // 2, some_push, 0)
    wait_blocks(landed2, NB - 1, rr2)
    ring2_out[...] = jnp.sum(landed2[...], axis=0)

    def send_ring2(d, _):
        copy(ring2_out, ring2.at[g], sg, rg, {"grp": (g + d) % G, "sub": s}).start()
        return 0

    lax.fori_loop(1, G, send_ring2, 0)
    ring2[g] = ring2_out[...]
    lax.fori_loop(count // 2, count, some_push, 0)
    ogvel[...] = bvel[...] + HALF * pushed()
    wait_blocks(ring2, G - 1, rg)
    ovel[...] = swap[last, s, 3:6, :] + HALF * jnp.sum(ring2[...], axis=0)[0:3]

    wait_blocks(stars, NB - 1, sa)
    wait_blocks(ring, Z - 1, sz)
    wait_sent(1 - last)
    wait_sent(last)
    wait_blocks(landed2, NB - 1, sr2)
    wait_blocks(ring2, G - 1, sg)


def solution(mesh):
    G = mesh.shape["grp"]
    NB = mesh.shape["sub"]
    Z = G
    X = NB // Z

    def local(cpos, cvel, cmass, gpos, gvel, gkind, species):
        bodies = gpos.shape[1]
        GB = bodies // LANES
        vmem = pl.BlockSpec(memory_space=pltpu.VMEM)
        smem = pl.BlockSpec(memory_space=pltpu.SMEM)
        dma = pltpu.SemaphoreType.DMA
        return pl.pallas_call(
            functools.partial(kernel, (G, X, Z, NB, GB)),
            out_shape=(
                jax.ShapeDtypeStruct(cpos.shape, F32),
                jax.ShapeDtypeStruct(cpos.shape, F32),
                jax.ShapeDtypeStruct(gpos.shape, F32),
                jax.ShapeDtypeStruct(gpos.shape, F32),
            ),
            in_specs=[vmem] * 6 + [smem],
            out_specs=(vmem,) * 4,
            scratch_shapes=[
                pltpu.VMEM((NB, 8, LANES), F32),
                pltpu.VMEM((4, bodies, LANES), F32),
                pltpu.VMEM((NB, 4, LANES), F32),
                pltpu.VMEM((NB, 4, LANES), F32),
                pltpu.VMEM((Z, 4, LANES), F32),
                pltpu.VMEM((4, LANES), F32),
                pltpu.VMEM((2, NB, 8, LANES), F32),
                pltpu.VMEM((NB, 4, LANES), F32),
                pltpu.VMEM((G, 4, LANES), F32),
                pltpu.VMEM((4, LANES), F32),
                pltpu.VMEM((6, LANES, LANES), F32),
                pltpu.VMEM((6, LANES, LANES), F32),
                pltpu.VMEM((3, bodies, LANES), F32),
                pltpu.VMEM((1, bodies), F32),
                pltpu.VMEM((3, bodies), F32),
                pltpu.VMEM((16, LANES), F32),
                dma, dma((Z // 2 + 1,)), dma, dma, dma, dma,
                dma((2,)), dma((2, X // 2 + G // 4 + 1)),
                dma, dma, dma, dma,
            ],
            compiler_params=pltpu.CompilerParams(collective_id=0, has_side_effects=True),
        )(cpos, cvel, cmass.reshape(1, LANES), gpos, gvel, gkind.reshape(1, bodies), species)

    return jax.shard_map(
        local,
        mesh=mesh,
        in_specs=(
            P(None, "sub"),
            P(None, "sub"),
            P("sub"),
            P(None, ("grp", "sub")),
            P(None, ("grp", "sub")),
            P(("grp", "sub")),
            P(),
        ),
        out_specs=(
            P(None, "sub"),
            P(None, "sub"),
            P(None, ("grp", "sub")),
            P(None, ("grp", "sub")),
        ),
        check_vma=False,
    )
```

```python
import functools

import jax
import jax.numpy as jnp
from jax import lax
from jax.experimental import pallas as pl
from jax.experimental.pallas import tpu as pltpu
from jax.sharding import PartitionSpec as P

SUBSTEPS = 8
STEP_TIME = 0.5
HALF = STEP_TIME / 2.0
BRIDGE_SOFT = 0.01
CLUSTER_SOFT = 0.0025
F32 = jnp.float32
BF16 = jnp.bfloat16
MESH = pl.DeviceIdType.MESH
LANES = 128


def ring_distance(d, n):
    return min(d % n, (-d) % n)


def chip_stages(X, Y):
    stages = [[] for _ in range(X // 2 + Y // 2 + 1)]
    for dx in range(X):
        for dy in range(Y):
            stages[ring_distance(dx, X) + ring_distance(dy, Y)].append((dx, dy))
    return stages


def halves(tile):
    high = tile.astype(BF16).astype(F32)
    return high, tile - high


def columns(tile):
    pad = jnp.zeros((LANES - tile.shape[0], LANES), F32)
    return jnp.concatenate([tile, pad], axis=0).T


def kernel(
    sizes,
    cpos, cvel, cmass, gpos, gvel, gkind, species,
    opos, ovel, ogpos, ogvel,
    stars, wide, bodies, ring, ring_out, swap, owned, owned_out,
    target, feature, weights, acc3, accj, accp, body, bvel, state,
    sa, ra, sb, rb, sz, rz, se, re, so, ro,
):
    G, X, Z, NB, GB = sizes
    total_bodies = GB * LANES * G * NB
    total_stars = NB * LANES
    g, s = lax.axis_index("grp"), lax.axis_index("sub")
    x, z = s // Z, s % Z
    q = x * G + g
    team = lambda p: {"grp": p % G, "sub": (p // G) * Z + z}
    Y, y, core = G // 2, g // 2, g % 2
    stages = chip_stages(X, Y)
    chip_at = lambda dx, dy: ((x + dx) % X) * G + ((y + dy) % Y) * 2

    def copy(src, dst, send, recv, dev):
        return pltpu.make_async_remote_copy(
            src_ref=src, dst_ref=dst, send_sem=send, recv_sem=recv,
            device_id=dev, device_id_type=MESH,
        )

    def wait_blocks(buf, n, sem):
        part = buf.at[pl.ds(0, n)]
        pltpu.make_async_copy(part, part, sem).wait()

    barrier = pltpu.get_barrier_semaphore()

    def greet_sub(d, _):
        pl.semaphore_signal(
            barrier, inc=1, device_id={"grp": g, "sub": (s + d) % NB}, device_id_type=MESH
        )
        return 0

    def greet_team(d, _):
        gd = (g + 1 + d // X) % G
        xd = d % X
        pl.semaphore_signal(
            barrier, inc=1, device_id={"grp": gd, "sub": xd * Z + z}, device_id_type=MESH
        )
        return 0

    for zs in range(Z):

        @pl.when((g != z) | (z != zs))
        def _():
            pl.semaphore_signal(
                barrier, inc=1, device_id={"grp": z, "sub": x * Z + zs}, device_id_type=MESH
            )

    lax.fori_loop(1, NB, greet_sub, 0)
    lax.fori_loop(0, (G - 1) * X, greet_team, 0)

    stars[s] = jnp.concatenate(
        [cpos[...], cmass[...] / total_stars, cvel[...], jnp.zeros((1, LANES), F32)], axis=0
    )
    kinds = gkind[...]
    mass = jnp.zeros(kinds.shape, F32)
    for kind in range(species.shape[0]):
        mass = mass + jnp.where(kinds == kind, species[kind], 0.0)
    body[...] = mass / total_bodies

    bodies[0, q] = jnp.concatenate([gpos[...], body[...]], axis=0)

    def widen(positions):
        for b in range(GB):
            cols = columns(positions[:, b * LANES : (b + 1) * LANES])
            for i in range(3):
                wide[i, b * LANES : (b + 1) * LANES, :] = jnp.broadcast_to(
                    cols[:, i : i + 1], (LANES, LANES)
                )

    swap[...] = jnp.ones(swap.shape, F32)

    own = (z == g).astype(jnp.int32)
    pl.semaphore_wait(barrier, (NB - 1) + (G - 1) * X + Z - own)

    def send_stars(dx, dz):
        to = {"grp": g, "sub": ((x + dx) % X) * Z + (z + dz) % Z}
        if dx == 0:
            copy(stars.at[s], stars.at[s], sa.at[0], ra.at[0], to).start()
        else:
            half = stars.at[s, pl.ds(0, 4)]
            copy(half, half, sa.at[1], ra.at[1], to).start()

    def wait_halves(sem):
        part = stars.at[pl.ds(0, (X - 1) * Z), pl.ds(0, 4)]
        pltpu.make_async_copy(part, part, sem).wait()

    def peers():
        for st in range(len(stages)):
            for dx, dy in stages[st]:
                for dc in range(2):
                    if (dx, dy, dc) != (0, 0, 0):
                        yield st, chip_at(dx, dy) + (core + dc) % 2

    def send_bodies(turn):
        for st, p in peers():
            copy(
                bodies.at[turn, q], bodies.at[turn, q], sb.at[turn], rb.at[turn, st], team(p)
            ).start()

    def wait_bodies(turn, count, sem):
        part = bodies.at[turn, pl.ds(0, count)]
        pltpu.make_async_copy(part, part, sem).wait()

    stage_size = [2 * len(chips) - (1 if st == 0 else 0) for st, chips in enumerate(stages)]

    for dz in range(1, Z):
        send_stars(0, dz)
    send_bodies(0)
    for dx in range(1, X):
        for dz in range(Z):
            send_stars(dx, dz)

    def set_position(rows):
        cols = columns(rows)
        for c in range(3):
            target[c] = jnp.broadcast_to(cols[:, c : c + 1], (LANES, LANES))

    def pull(at, acc, row):
        for i in range(len(row)):
            d = [row[i][c] - at[c] for c in range(3)]
            r2 = d[0] * d[0] + d[1] * d[1] + d[2] * d[2] + BRIDGE_SOFT
            inv = lax.rsqrt(r2)
            w = row[i][3] * (inv * inv * inv)
            acc = tuple(acc[c] + w * d[c] for c in range(3))
        return acc

    def pull_rows(body_of, first):
        def rows32(i, _):
            here = pl.ds(pl.multiple_of(i * 32, 32), 32)
            at = [target[c, here, :] for c in range(3)]
            if first:
                acc = (jnp.zeros((32, LANES), F32),) * 3
            else:
                acc = tuple(acc3[c, here, :] for c in range(3))
            acc = body_of(at, acc)
            for c in range(3):
                acc3[c, here, :] = acc[c]
            return 0

        lax.fori_loop(0, LANES // 32, rows32, 0)

    def lanes_of(turn, b, l):
        return [bodies[turn, b, c : c + 1, pl.ds(l * LANES, LANES)] for c in range(4)]

    def pull_stage(turn, st):
        blocks = [chip_at(dx, dy) + c for dx, dy in stages[st] for c in range(2)]

        def some(at, acc):
            def lane(l, acc):
                l = pl.multiple_of(l * LANES, LANES)
                rows = [
                    [bodies[turn, b, c : c + 1, pl.ds(l, LANES)] for c in range(4)] for b in blocks
                ]
                return pull(at, acc, rows)

            return lax.fori_loop(0, GB, lane, acc)

        pull_rows(some, st == 0)

    def pull_all(turn):
        def some(at, acc):
            def one(b, acc):
                return pull(at, acc, [lanes_of(turn, b, l) for l in range(GB)])

            return lax.fori_loop(0, NB, one, acc)

        pull_rows(some, True)

    def pulled():
        return jnp.concatenate(
            [jnp.sum(acc3[c].T, axis=0, keepdims=True) for c in range(3)]
            + [jnp.zeros((1, LANES), F32)],
            axis=0,
        )

    def push(first, position_row):
        here = pl.ds(pl.multiple_of(first, 16), 16)
        at = [wide[c, here, :] for c in range(3)]

        def step(b, acc):
            d = [position_row(b, c) - at[c] for c in range(3)]
            r2 = d[0] * d[0] + d[1] * d[1] + d[2] * d[2] + BRIDGE_SOFT
            inv = lax.rsqrt(r2)
            w = stars[b, 3:4, :] * (inv * inv * inv)
            return tuple(acc[c] + w * d[c] for c in range(3))

        zero = jnp.zeros((16, LANES), F32)
        acc = lax.fori_loop(0, NB, step, (zero, zero, zero), unroll=4)
        for c in range(3):
            accp[c, here, :] = acc[c]

    def pushed():
        rows = []
        for c in range(3):
            rows.append(
                jnp.concatenate(
                    [
                        jnp.sum(accp[c, b * LANES : (b + 1) * LANES, :].T, axis=0, keepdims=True)
                        for b in range(GB)
                    ],
                    axis=1,
                )
            )
        return jnp.concatenate(rows, axis=0)

    widen(gpos[...])
    wait_blocks(stars, Z - 1, ra.at[0])
    set_position(stars[q, 0:3, :])
    for st in range(len(stages)):
        wait_bodies(0, stage_size[st], rb.at[0, st])
        pull_stage(0, st)
    ring_out[...] = pulled()

    def send_ring(d, _):
        copy(ring_out, ring.at[z], sz, rz, {"grp": g, "sub": x * Z + (z + d) % Z}).start()
        return 0

    lax.fori_loop(1, Z, send_ring, 0)
    ring[z] = ring_out[...]
    wait_halves(ra.at[1])
    wait_blocks(ring, Z - 1, rz)
    mine = stars[q]
    state[0:3, :] = mine[0:3]
    state[3:6, :] = mine[4:7] + HALF * jnp.sum(ring[...], axis=0)[0:3]
    state[6:12, :] = jnp.zeros((6, LANES), F32)

    one_row = jnp.ones((1, LANES), F32)
    row6 = lax.broadcasted_iota(jnp.int32, (8, LANES), 0) == 6
    none8 = jnp.zeros((8, LANES), F32)
    none16 = jnp.zeros((16, 2 * LANES), BF16)

    def dotted(rows):
        return jnp.sum(rows[0:3] * rows[3:6], axis=0, keepdims=True)

    def send_swap(par, rows):
        swap[par, q, 0:6, :] = rows
        for st, p in peers():
            copy(
                swap.at[par, q, pl.ds(0, 6)], swap.at[par, q, pl.ds(0, 6)],
                se.at[par], re.at[par, st], team(p),
            ).start()

    def wait_swap(par, sem, count):
        part = swap.at[par, pl.ds(0, count), pl.ds(0, 6)]
        pltpu.make_async_copy(part, part, sem).wait()

    def wait_sent(par):
        wait_swap(par, se.at[par], NB - 1)

    def wait_stage(par, st):
        wait_swap(par, re.at[par, st], stage_size[st])

    def set_target(rows):
        coef = jnp.concatenate([-rows[3:6], -rows[0:3], one_row, dotted(rows)], axis=0)
        high, low = halves(coef)
        cols = columns(jnp.concatenate([high, high, low, none8, rows[0:3]], axis=0))
        feature[...] = cols[:, 0:32].astype(BF16)
        for c in range(3):
            target[c] = jnp.broadcast_to(cols[:, 32 + c : 33 + c], (LANES, LANES))

    def rates_chip(par, chip, first, slot):
        sources, sums = [], []
        for k in range(2):
            tile = swap[par, chip + k]
            tile = jnp.where(row6, dotted(tile), tile)
            high, low = halves(tile)
            sources.append(jnp.concatenate([high, low, high, none8], axis=0).astype(BF16))
            high, low = halves(tile * stars[chip + k, 3:4, :])
            sums.append(jnp.concatenate([high, low], axis=0).astype(BF16))
        sums = jnp.concatenate(sums, axis=1)
        both = jnp.concatenate(
            [
                jnp.concatenate([sums, none16], axis=1),
                jnp.concatenate([none16, sums], axis=1),
            ],
            axis=0,
        )
        rv = jnp.dot(
            feature[...], jnp.concatenate(sources, axis=1), preferred_element_type=F32
        )
        for i in range(LANES // 16):
            here = slice(i * 16, (i + 1) * 16)
            at = [target[c, here, :] for c in range(3)]
            if first:
                acc = [jnp.zeros((16, LANES), F32)] * 3
            else:
                acc = [acc3[c, here, :] for c in range(3)]
            for k in range(2):
                b = chip + k
                lanes = slice(k * LANES, (k + 1) * LANES)
                d = [swap[par, b, c : c + 1, :] - at[c] for c in range(3)]
                r2 = d[0] * d[0] + d[1] * d[1] + d[2] * d[2] + CLUSTER_SOFT
                inv = lax.rsqrt(r2)
                i2 = inv * inv
                w = inv * i2
                mw = stars[b, 3:4, :] * w
                acc = [acc[c] + mw * d[c] for c in range(3)]
                weights[slot, here, lanes] = w.astype(BF16)
                u = (w * i2) * rv[here, lanes]
                weights[slot, here, 2 * LANES + k * LANES : 3 * LANES + k * LANES] = u.astype(BF16)
            for c in range(3):
                acc3[c, here, :] = acc[c]
        out = lax.dot_general(
            weights[slot], both, (((1,), (1,)), ((), ())), preferred_element_type=F32
        )
        accj[...] = out if first else accj[...] + out

    def rates(par, rows):
        turn = 0
        for st, chips in enumerate(stages):
            wait_stage(par, st)
            for dx, dy in chips:
                rates_chip(par, chip_at(dx, dy), turn == 0, turn % 2)
                turn += 1
        a = jnp.concatenate(
            [jnp.sum(acc3[c].T, axis=0, keepdims=True) for c in range(3)], axis=0
        )
        sums = jnp.concatenate([accj[...], jnp.zeros((LANES, LANES - 32), F32)], axis=1).T
        of_w = sums[0:8] + sums[8:16]
        of_u = sums[16:24] + sums[24:32]
        j = (of_w[3:6] - rows[3:6] * of_w[7:8]) - 3.0 * (of_u[0:3] - rows[0:3] * of_u[7:8])
        return jnp.concatenate([a, j], axis=0)

    h = STEP_TIME / SUBSTEPS

    def substep(k, _):
        par = k % 2
        first = k == 0
        xs, v, a, j = state[0:3, :], state[3:6, :], state[6:9, :], state[9:12, :]
        guess = jnp.concatenate(
            [
                xs + h * (v + h * (a / 2.0 + h * j / 6.0)),
                v + h * (a + h * j / 2.0),
            ],
            axis=0,
        )
        rows = jnp.where(first, state[0:6, :], guess)

        @pl.when(k >= 2)
        def _():
            wait_sent(par)

        send_swap(par, rows)
        set_target(rows)

        @pl.when(k < SUBSTEPS)
        def _():
            count = GB * LANES // SUBSTEPS

            def some(i, _):
                push(k * count + i * 16, lambda b, c: stars[b, c : c + 1, :])
                return 0

            lax.fori_loop(0, count // 16, some, 0)

        @pl.when(k == SUBSTEPS)
        def _():
            velocity = gvel[...] + HALF * pushed()
            bvel[...] = velocity
            moved = gpos[...] + STEP_TIME * velocity
            ogpos[...] = moved
            bodies[1, q] = jnp.concatenate([moved, body[...]], axis=0)
            send_bodies(1)
            widen(moved)

        fresh = rates(par, rows)
        a1, j1 = fresh[0:3], fresh[3:6]
        v1 = v + h / 2.0 * (a + a1) + h * h / 12.0 * (j - j1)
        x1 = xs + h / 2.0 * (v + v1) + h * h / 12.0 * (a - a1)
        state[0:3, :] = jnp.where(first, xs, x1)
        state[3:6, :] = jnp.where(first, v, v1)
        state[6:9, :] = a1
        state[9:12, :] = j1
        return 0

    lax.fori_loop(0, SUBSTEPS + 1, substep, 0)

    last = (SUBSTEPS + 1) % 2
    wait_sent(last)
    send_swap(last, state[0:6, :])
    set_position(state[0:3, :])
    for st in range(len(stages)):
        wait_bodies(1, stage_size[st], rb.at[1, st])
    pull_all(1)
    owned_out[...] = pulled()

    for gg in range(G):

        @pl.when((g != gg) | (z != g))
        def _():
            copy(owned_out, owned.at[z], so, ro, {"grp": gg, "sub": x * Z + g}).start()

    @pl.when(z == g)
    def _():
        owned[z] = owned_out[...]

    for st in range(len(stages)):
        wait_stage(last, st)
    opos[...] = swap[last, s, 0:3, :]

    def some_push(i, _):
        push(i * 16, lambda b, c: swap[last, b, c : c + 1, :])
        return 0

    lax.fori_loop(0, GB * LANES // 16, some_push, 0)
    ogvel[...] = bvel[...] + HALF * pushed()

    @pl.when(z == g)
    def _():
        wait_blocks(owned, Z - 1, ro)
        wait_blocks(owned, Z - 1, so)

    @pl.when(z != g)
    def _():
        wait_blocks(owned, Z, ro)
        wait_blocks(owned, Z, so)

    ovel[...] = swap[last, s, 3:6, :] + HALF * jnp.sum(owned[...], axis=0)[0:3]

    wait_blocks(stars, Z - 1, sa.at[0])
    wait_halves(sa.at[1])
    wait_blocks(ring, Z - 1, sz)
    for turn in range(2):
        wait_bodies(turn, NB - 1, sb.at[turn])
    wait_sent(1 - last)
    wait_sent(last)


def hand_on(*refs):
    for source, result in zip(refs[:4], refs[4:]):
        result[...] = source[...]


def solution(mesh):
    G = mesh.shape["grp"]
    NB = mesh.shape["sub"]
    Z = G
    X = NB // Z

    def local(cpos, cvel, cmass, gpos, gvel, gkind, species):
        bodies = gpos.shape[1]
        GB = bodies // LANES
        stages = len(chip_stages(X, G // 2))
        vmem = pl.BlockSpec(memory_space=pltpu.VMEM)
        smem = pl.BlockSpec(memory_space=pltpu.SMEM)
        dma = pltpu.SemaphoreType.DMA
        shapes = (
            jax.ShapeDtypeStruct(cpos.shape, F32),
            jax.ShapeDtypeStruct(cpos.shape, F32),
            jax.ShapeDtypeStruct(gpos.shape, F32),
            jax.ShapeDtypeStruct(gpos.shape, F32),
        )
        results = pl.pallas_call(
            functools.partial(kernel, (G, X, Z, NB, GB)),
            out_shape=shapes,
            in_specs=[vmem] * 6 + [smem],
            out_specs=(vmem,) * 4,
            scratch_shapes=[
                pltpu.VMEM((NB, 8, LANES), F32),
                pltpu.VMEM((3, bodies, LANES), F32),
                pltpu.VMEM((2, NB, 4, bodies), F32),
                pltpu.VMEM((Z, 4, LANES), F32),
                pltpu.VMEM((4, LANES), F32),
                pltpu.VMEM((2, NB, 8, LANES), F32),
                pltpu.VMEM((Z, 4, LANES), F32),
                pltpu.VMEM((4, LANES), F32),
                pltpu.VMEM((3, LANES, LANES), F32),
                pltpu.VMEM((LANES, 32), BF16),
                pltpu.VMEM((2, LANES, 4 * LANES), BF16),
                pltpu.VMEM((3, LANES, LANES), F32),
                pltpu.VMEM((LANES, 32), F32),
                pltpu.VMEM((3, bodies, LANES), F32),
                pltpu.VMEM((1, bodies), F32),
                pltpu.VMEM((3, bodies), F32),
                pltpu.VMEM((16, LANES), F32),
                dma((2,)), dma((2,)), dma((2,)), dma((2, stages)), dma, dma,
                dma((2,)), dma((2, stages)), dma, dma,
            ],
            compiler_params=pltpu.CompilerParams(collective_id=0, has_side_effects=True),
        )(cpos, cvel, cmass.reshape(1, LANES), gpos, gvel, gkind.reshape(1, bodies), species)
        return pl.pallas_call(
            hand_on, out_shape=shapes, in_specs=[vmem] * 4, out_specs=(vmem,) * 4
        )(*results)

    return jax.shard_map(
        local,
        mesh=mesh,
        in_specs=(
            P(None, "sub"),
            P(None, "sub"),
            P("sub"),
            P(None, ("grp", "sub")),
            P(None, ("grp", "sub")),
            P(("grp", "sub")),
            P(),
        ),
        out_specs=(
            P(None, "sub"),
            P(None, "sub"),
            P(None, ("grp", "sub")),
            P(None, ("grp", "sub")),
        ),
        check_vma=False,
    )
```

```python
import functools

import jax
import jax.numpy as jnp
from jax import lax
from jax.experimental import pallas as pl
from jax.experimental.pallas import tpu as pltpu
from jax.sharding import PartitionSpec as P

SUBSTEPS = 8
STEP_TIME = 0.5
HALF = STEP_TIME / 2.0
BRIDGE_SOFT = 0.01
CLUSTER_SOFT = 0.0025
F32 = jnp.float32
BF16 = jnp.bfloat16
MESH = pl.DeviceIdType.MESH
LANES = 128


def ring_distance(d, n):
    return min(d % n, (-d) % n)


def chip_stages(X, Y):
    stages = [[] for _ in range(X // 2 + Y // 2 + 1)]
    for dx in range(X):
        for dy in range(Y):
            stages[ring_distance(dx, X) + ring_distance(dy, Y)].append((dx, dy))
    return stages


def halves(tile):
    high = tile.astype(BF16).astype(F32)
    return high, tile - high


def columns(tile):
    pad = jnp.zeros((LANES - tile.shape[0], LANES), F32)
    return jnp.concatenate([tile, pad], axis=0).T


def kernel(
    sizes,
    cpos, cvel, cmass, gpos, gvel, gkind, species,
    opos, ovel, ogpos, ogvel,
    stars, wide, bodies, ring, ring_out, swap, owned, owned_out,
    target, feature, weights, acc3, accj, accp, body, bvel, state,
    sa, ra, sb, rb, sz, rz, se, re, so, ro,
):
    G, X, Z, NB, GB = sizes
    total_bodies = GB * LANES * G * NB
    total_stars = NB * LANES
    g, s = lax.axis_index("grp"), lax.axis_index("sub")
    x, z = s // Z, s % Z
    q = x * G + g
    team = lambda p: {"grp": p % G, "sub": (p // G) * Z + z}
    Y, y, core = G // 2, g // 2, g % 2
    stages = chip_stages(X, Y)
    chip_at = lambda dx, dy: ((x + dx) % X) * G + ((y + dy) % Y) * 2

    def copy(src, dst, send, recv, dev):
        return pltpu.make_async_remote_copy(
            src_ref=src, dst_ref=dst, send_sem=send, recv_sem=recv,
            device_id=dev, device_id_type=MESH,
        )

    def wait_blocks(buf, n, sem):
        part = buf.at[pl.ds(0, n)]
        pltpu.make_async_copy(part, part, sem).wait()

    barrier = pltpu.get_barrier_semaphore()

    def greet_sub(d, _):
        pl.semaphore_signal(
            barrier, inc=1, device_id={"grp": g, "sub": (s + d) % NB}, device_id_type=MESH
        )
        return 0

    def greet_team(d, _):
        gd = (g + 1 + d // X) % G
        xd = d % X
        pl.semaphore_signal(
            barrier, inc=1, device_id={"grp": gd, "sub": xd * Z + z}, device_id_type=MESH
        )
        return 0

    for zs in range(Z):

        @pl.when((g != z) | (z != zs))
        def _():
            pl.semaphore_signal(
                barrier, inc=1, device_id={"grp": z, "sub": x * Z + zs}, device_id_type=MESH
            )

    lax.fori_loop(1, NB, greet_sub, 0)
    lax.fori_loop(0, (G - 1) * X, greet_team, 0)

    stars[s] = jnp.concatenate(
        [cpos[...], cmass[...] / total_stars, cvel[...], jnp.zeros((1, LANES), F32)], axis=0
    )
    kinds = gkind[...]
    mass = jnp.zeros(kinds.shape, F32)
    for kind in range(species.shape[0]):
        mass = mass + jnp.where(kinds == kind, species[kind], 0.0)
    body[...] = mass / total_bodies

    bodies[0, q] = jnp.concatenate([gpos[...], body[...]], axis=0)

    def widen(positions):
        for b in range(GB):
            cols = columns(positions[:, b * LANES : (b + 1) * LANES])
            for i in range(3):
                wide[i, b * LANES : (b + 1) * LANES, :] = jnp.broadcast_to(
                    cols[:, i : i + 1], (LANES, LANES)
                )

    swap[...] = jnp.ones(swap.shape, F32)

    own = (z == g).astype(jnp.int32)
    pl.semaphore_wait(barrier, (NB - 1) + (G - 1) * X + Z - own)

    def send_stars(dx, dz):
        to = {"grp": g, "sub": ((x + dx) % X) * Z + (z + dz) % Z}
        if dx == 0:
            copy(stars.at[s], stars.at[s], sa.at[0], ra.at[0], to).start()
        else:
            half = stars.at[s, pl.ds(0, 4)]
            copy(half, half, sa.at[1], ra.at[1], to).start()

    def wait_halves(sem):
        part = stars.at[pl.ds(0, (X - 1) * Z), pl.ds(0, 4)]
        pltpu.make_async_copy(part, part, sem).wait()

    def peers():
        for st in range(len(stages)):
            for dx, dy in stages[st]:
                for dc in range(2):
                    if (dx, dy, dc) != (0, 0, 0):
                        yield st, chip_at(dx, dy) + (core + dc) % 2

    def send_bodies(turn):
        for st, p in peers():
            copy(
                bodies.at[turn, q], bodies.at[turn, q], sb.at[turn], rb.at[turn, st], team(p)
            ).start()

    def wait_bodies(turn, count, sem):
        part = bodies.at[turn, pl.ds(0, count)]
        pltpu.make_async_copy(part, part, sem).wait()

    stage_size = [2 * len(chips) - (1 if st == 0 else 0) for st, chips in enumerate(stages)]

    for dz in range(1, Z):
        send_stars(0, dz)
    send_bodies(0)
    for dx in range(1, X):
        for dz in range(Z):
            send_stars(dx, dz)

    def set_position(rows):
        cols = columns(rows)
        for c in range(3):
            target[c] = jnp.broadcast_to(cols[:, c : c + 1], (LANES, LANES))

    def pull(at, acc, row):
        for i in range(len(row)):
            d = [row[i][c] - at[c] for c in range(3)]
            r2 = d[0] * d[0] + d[1] * d[1] + d[2] * d[2] + BRIDGE_SOFT
            inv = lax.rsqrt(r2)
            w = row[i][3] * (inv * inv * inv)
            acc = tuple(acc[c] + w * d[c] for c in range(3))
        return acc

    def pull_rows(body_of, first):
        def rows32(i, _):
            here = pl.ds(pl.multiple_of(i * 32, 32), 32)
            at = [target[c, here, :] for c in range(3)]
            if first:
                acc = (jnp.zeros((32, LANES), F32),) * 3
            else:
                acc = tuple(acc3[c, here, :] for c in range(3))
            acc = body_of(at, acc)
            for c in range(3):
                acc3[c, here, :] = acc[c]
            return 0

        lax.fori_loop(0, LANES // 32, rows32, 0)

    def lanes_of(turn, b, l):
        return [bodies[turn, b, c : c + 1, pl.ds(l * LANES, LANES)] for c in range(4)]

    def pull_stage(turn, st):
        blocks = [chip_at(dx, dy) + c for dx, dy in stages[st] for c in range(2)]

        def some(at, acc):
            def lane(l, acc):
                l = pl.multiple_of(l * LANES, LANES)
                rows = [
                    [bodies[turn, b, c : c + 1, pl.ds(l, LANES)] for c in range(4)] for b in blocks
                ]
                return pull(at, acc, rows)

            return lax.fori_loop(0, GB, lane, acc)

        pull_rows(some, st == 0)

    def pull_all(turn):
        def some(at, acc):
            def one(b, acc):
                return pull(at, acc, [lanes_of(turn, b, l) for l in range(GB)])

            return lax.fori_loop(0, NB, one, acc, unroll=2)

        pull_rows(some, True)

    def pulled():
        return jnp.concatenate(
            [jnp.sum(acc3[c].T, axis=0, keepdims=True) for c in range(3)]
            + [jnp.zeros((1, LANES), F32)],
            axis=0,
        )

    def push(first, position_row):
        here = pl.ds(pl.multiple_of(first, 32), 32)
        at = [wide[c, here, :] for c in range(3)]

        def step(b, acc):
            d = [position_row(b, c) - at[c] for c in range(3)]
            r2 = d[0] * d[0] + d[1] * d[1] + d[2] * d[2] + BRIDGE_SOFT
            inv = lax.rsqrt(r2)
            w = stars[b, 3:4, :] * (inv * inv * inv)
            return tuple(acc[c] + w * d[c] for c in range(3))

        zero = jnp.zeros((32, LANES), F32)
        acc = lax.fori_loop(0, NB, step, (zero, zero, zero), unroll=4)
        for c in range(3):
            accp[c, here, :] = acc[c]

    def pushed():
        rows = []
        for c in range(3):
            rows.append(
                jnp.concatenate(
                    [
                        jnp.sum(accp[c, b * LANES : (b + 1) * LANES, :].T, axis=0, keepdims=True)
                        for b in range(GB)
                    ],
                    axis=1,
                )
            )
        return jnp.concatenate(rows, axis=0)

    widen(gpos[...])
    wait_blocks(stars, Z - 1, ra.at[0])
    set_position(stars[q, 0:3, :])
    for st in range(len(stages)):
        wait_bodies(0, stage_size[st], rb.at[0, st])
        pull_stage(0, st)
    ring_out[...] = pulled()

    def send_ring(d, _):
        copy(ring_out, ring.at[z], sz, rz, {"grp": g, "sub": x * Z + (z + d) % Z}).start()
        return 0

    lax.fori_loop(1, Z, send_ring, 0)
    ring[z] = ring_out[...]
    wait_halves(ra.at[1])
    wait_blocks(ring, Z - 1, rz)
    mine = stars[q]
    state[0:3, :] = mine[0:3]
    state[3:6, :] = mine[4:7] + HALF * jnp.sum(ring[...], axis=0)[0:3]
    state[6:12, :] = jnp.zeros((6, LANES), F32)

    one_row = jnp.ones((1, LANES), F32)
    row6 = lax.broadcasted_iota(jnp.int32, (8, LANES), 0) == 6
    none8 = jnp.zeros((8, LANES), F32)
    none16 = jnp.zeros((16, 2 * LANES), BF16)

    def dotted(rows):
        return jnp.sum(rows[0:3] * rows[3:6], axis=0, keepdims=True)

    def send_swap(par, rows):
        swap[par, q, 0:6, :] = rows
        for st, p in peers():
            copy(
                swap.at[par, q, pl.ds(0, 6)], swap.at[par, q, pl.ds(0, 6)],
                se.at[par], re.at[par, st], team(p),
            ).start()

    def wait_swap(par, sem, count):
        part = swap.at[par, pl.ds(0, count), pl.ds(0, 6)]
        pltpu.make_async_copy(part, part, sem).wait()

    def wait_sent(par):
        wait_swap(par, se.at[par], NB - 1)

    def wait_stage(par, st):
        wait_swap(par, re.at[par, st], stage_size[st])

    def set_target(rows):
        coef = jnp.concatenate([-rows[3:6], -rows[0:3], one_row, dotted(rows)], axis=0)
        high, low = halves(coef)
        cols = columns(jnp.concatenate([high, high, low, none8, rows[0:3]], axis=0))
        feature[...] = cols[:, 0:32].astype(BF16)
        for c in range(3):
            target[c] = jnp.broadcast_to(cols[:, 32 + c : 33 + c], (LANES, LANES))

    def rates_chip(par, chip, first, slot, base):
        sources, sums = [], []
        for k in range(2):
            tile = swap[par, chip + k]
            tile = jnp.where(row6, dotted(tile), tile)
            high, low = halves(tile)
            sources.append(jnp.concatenate([high, low, high, none8], axis=0).astype(BF16))
            high, low = halves(tile * stars[chip + k, 3:4, :])
            sums.append(jnp.concatenate([high, low], axis=0).astype(BF16))
        sums = jnp.concatenate(sums, axis=1)
        both = jnp.concatenate(
            [
                jnp.concatenate([sums, none16], axis=1),
                jnp.concatenate([none16, sums], axis=1),
            ],
            axis=0,
        )
        rv = jnp.dot(
            feature[...], jnp.concatenate(sources, axis=1), preferred_element_type=F32
        )
        for i in range(LANES // 16):
            here = slice(i * 16, (i + 1) * 16)
            at = [target[c, here, :] for c in range(3)]
            if first:
                acc = [jnp.zeros((16, LANES), F32)] * 3
            else:
                acc = [acc3[c, here, :] for c in range(3)]
            for k in range(2):
                b = chip + k
                lanes = slice(k * LANES, (k + 1) * LANES)
                d = [swap[par, b, c : c + 1, :] - at[c] for c in range(3)]
                r2 = d[0] * d[0] + d[1] * d[1] + d[2] * d[2] + CLUSTER_SOFT
                inv = lax.rsqrt(r2)
                i2 = inv * inv
                w = inv * i2
                mw = stars[b, 3:4, :] * w
                acc = [acc[c] + mw * d[c] for c in range(3)]
                weights[slot, here, base + k * LANES : base + (k + 1) * LANES] = w.astype(BF16)
                u = (w * i2) * rv[here, lanes]
                weights[slot, here, base + (2 + k) * LANES : base + (3 + k) * LANES] = u.astype(BF16)
            for c in range(3):
                acc3[c, here, :] = acc[c]
        return both

    def rates(par, rows):
        for st, chips in enumerate(stages):
            wait_stage(par, st)
            both = [
                rates_chip(par, chip_at(dx, dy), st == 0, st % 2, i * 4 * LANES)
                for i, (dx, dy) in enumerate(chips)
            ]
            out = lax.dot_general(
                weights[st % 2, :, 0 : len(chips) * 4 * LANES], jnp.concatenate(both, axis=1),
                (((1,), (1,)), ((), ())), preferred_element_type=F32,
            )
            accj[...] = out if st == 0 else accj[...] + out
        a = jnp.concatenate(
            [jnp.sum(acc3[c].T, axis=0, keepdims=True) for c in range(3)], axis=0
        )
        sums = jnp.concatenate([accj[...], jnp.zeros((LANES, LANES - 32), F32)], axis=1).T
        of_w = sums[0:8] + sums[8:16]
        of_u = sums[16:24] + sums[24:32]
        j = (of_w[3:6] - rows[3:6] * of_w[7:8]) - 3.0 * (of_u[0:3] - rows[0:3] * of_u[7:8])
        return jnp.concatenate([a, j], axis=0)

    h = STEP_TIME / SUBSTEPS

    def substep(k, _):
        par = k % 2
        first = k == 0
        xs, v, a, j = state[0:3, :], state[3:6, :], state[6:9, :], state[9:12, :]
        guess = jnp.concatenate(
            [
                xs + h * (v + h * (a / 2.0 + h * j / 6.0)),
                v + h * (a + h * j / 2.0),
            ],
            axis=0,
        )
        rows = jnp.where(first, state[0:6, :], guess)

        @pl.when(k >= 2)
        def _():
            wait_sent(par)

        send_swap(par, rows)
        set_target(rows)

        @pl.when(k < SUBSTEPS)
        def _():
            count = GB * LANES // SUBSTEPS

            def some(i, _):
                push(k * count + i * 32, lambda b, c: stars[b, c : c + 1, :])
                return 0

            lax.fori_loop(0, count // 32, some, 0)

        @pl.when(k == SUBSTEPS)
        def _():
            velocity = gvel[...] + HALF * pushed()
            bvel[...] = velocity
            moved = gpos[...] + STEP_TIME * velocity
            ogpos[...] = moved
            bodies[1, q] = jnp.concatenate([moved, body[...]], axis=0)
            send_bodies(1)
            widen(moved)

        fresh = rates(par, rows)
        a1, j1 = fresh[0:3], fresh[3:6]
        v1 = v + h / 2.0 * (a + a1) + h * h / 12.0 * (j - j1)
        x1 = xs + h / 2.0 * (v + v1) + h * h / 12.0 * (a - a1)
        state[0:3, :] = jnp.where(first, xs, x1)
        state[3:6, :] = jnp.where(first, v, v1)
        state[6:9, :] = a1
        state[9:12, :] = j1
        return 0

    lax.fori_loop(0, SUBSTEPS + 1, substep, 0)

    last = (SUBSTEPS + 1) % 2
    wait_sent(last)
    send_swap(last, state[0:6, :])
    set_position(state[0:3, :])
    for st in range(len(stages)):
        wait_bodies(1, stage_size[st], rb.at[1, st])
    pull_all(1)
    owned_out[...] = pulled()

    for gg in range(G):

        @pl.when((g != gg) | (z != g))
        def _():
            copy(owned_out, owned.at[z], so, ro, {"grp": gg, "sub": x * Z + g}).start()

    @pl.when(z == g)
    def _():
        owned[z] = owned_out[...]

    for st in range(len(stages)):
        wait_stage(last, st)
    opos[...] = swap[last, s, 0:3, :]

    def some_push(i, _):
        push(i * 32, lambda b, c: swap[last, b, c : c + 1, :])
        return 0

    lax.fori_loop(0, GB * LANES // 32, some_push, 0)
    ogvel[...] = bvel[...] + HALF * pushed()

    @pl.when(z == g)
    def _():
        wait_blocks(owned, Z - 1, ro)
        wait_blocks(owned, Z - 1, so)

    @pl.when(z != g)
    def _():
        wait_blocks(owned, Z, ro)
        wait_blocks(owned, Z, so)

    ovel[...] = swap[last, s, 3:6, :] + HALF * jnp.sum(owned[...], axis=0)[0:3]

    wait_blocks(stars, Z - 1, sa.at[0])
    wait_halves(sa.at[1])
    wait_blocks(ring, Z - 1, sz)
    for turn in range(2):
        wait_bodies(turn, NB - 1, sb.at[turn])
    wait_sent(1 - last)
    wait_sent(last)


def hand_on(*refs):
    for source, result in zip(refs[:4], refs[4:]):
        result[...] = source[...]


def solution(mesh):
    G = mesh.shape["grp"]
    NB = mesh.shape["sub"]
    Z = G
    X = NB // Z

    def local(cpos, cvel, cmass, gpos, gvel, gkind, species):
        bodies = gpos.shape[1]
        GB = bodies // LANES
        stages = len(chip_stages(X, G // 2))
        longest = max(len(chips) for chips in chip_stages(X, G // 2))
        vmem = pl.BlockSpec(memory_space=pltpu.VMEM)
        smem = pl.BlockSpec(memory_space=pltpu.SMEM)
        dma = pltpu.SemaphoreType.DMA
        shapes = (
            jax.ShapeDtypeStruct(cpos.shape, F32),
            jax.ShapeDtypeStruct(cpos.shape, F32),
            jax.ShapeDtypeStruct(gpos.shape, F32),
            jax.ShapeDtypeStruct(gpos.shape, F32),
        )
        results = pl.pallas_call(
            functools.partial(kernel, (G, X, Z, NB, GB)),
            out_shape=shapes,
            in_specs=[vmem] * 6 + [smem],
            out_specs=(vmem,) * 4,
            scratch_shapes=[
                pltpu.VMEM((NB, 8, LANES), F32),
                pltpu.VMEM((3, bodies, LANES), F32),
                pltpu.VMEM((2, NB, 4, bodies), F32),
                pltpu.VMEM((Z, 4, LANES), F32),
                pltpu.VMEM((4, LANES), F32),
                pltpu.VMEM((2, NB, 8, LANES), F32),
                pltpu.VMEM((Z, 4, LANES), F32),
                pltpu.VMEM((4, LANES), F32),
                pltpu.VMEM((3, LANES, LANES), F32),
                pltpu.VMEM((LANES, 32), BF16),
                pltpu.VMEM((2, LANES, longest * 4 * LANES), BF16),
                pltpu.VMEM((3, LANES, LANES), F32),
                pltpu.VMEM((LANES, 32), F32),
                pltpu.VMEM((3, bodies, LANES), F32),
                pltpu.VMEM((1, bodies), F32),
                pltpu.VMEM((3, bodies), F32),
                pltpu.VMEM((16, LANES), F32),
                dma((2,)), dma((2,)), dma((2,)), dma((2, stages)), dma, dma,
                dma((2,)), dma((2, stages)), dma, dma,
            ],
            compiler_params=pltpu.CompilerParams(collective_id=0, has_side_effects=True),
        )(cpos, cvel, cmass.reshape(1, LANES), gpos, gvel, gkind.reshape(1, bodies), species)
        return pl.pallas_call(
            hand_on, out_shape=shapes, in_specs=[vmem] * 4, out_specs=(vmem,) * 4
        )(*results)

    return jax.shard_map(
        local,
        mesh=mesh,
        in_specs=(
            P(None, "sub"),
            P(None, "sub"),
            P("sub"),
            P(None, ("grp", "sub")),
            P(None, ("grp", "sub")),
            P(("grp", "sub")),
            P(),
        ),
        out_specs=(
            P(None, "sub"),
            P(None, "sub"),
            P(None, ("grp", "sub")),
            P(None, ("grp", "sub")),
        ),
        check_vma=False,
    )
```
